32 devices in a mesh: con: 4 (over x, core), res: 8 (over z, y).
Axes of the slice: x: 2, y: 2, z: 4, core: 2. Of those that a mesh axis runs over, the one named last changes fastest.
Arguments:
- integrals: float32 [24576, 24576], P('res', 'con'), as said below
- tile_mask: int32 [96, 96], P('res', 'con'), may hold values from 0 to 1, as said below
- amplitudes: float32 [24576, 384], P(('con', 'res')), may hold values from -4 to 4
- other_first: float32 [24576, 384], P(('res', 'con')), may hold values from -6 to 6
- other_second: float32 [24576, 384], P(('con', 'res')), may hold values from -6 to 6
- vir_index: int32 [2, 24576], replicated, may hold values from 0 to 1599
- occ_index: int32 [2, 384], replicated, may hold values from 0 to 31, as said below
- partner: int32 [384], replicated, may hold values from 0 to 383, as said below
- eps_vir: float32 [1600], replicated, may hold values from 0.2 to 3
- eps_occ: float32 [32], replicated, may hold values from -2 to -0.2
Outputs:
- first_update: float32 [24576, 384], P(('res', 'con'))
- second_update: float32 [24576, 384], P(('con', 'res'))
The draws below stay inside these ranges and needn't reach their ends.
Inputs may be any that keep to these rules, and one draw needn't show every extreme that they name: integrals is symmetric: integrals[p, s] == integrals[s, p]. tile_mask is symmetric and its diagonal is 1. partner is a permutation that is its own inverse with no fixed point. The two orbitals of an occupied pair differ, and occ_index[0, partner[q]] == occ_index[1, q].
All inputs are finite; a program needn't handle non-finite values.
Results may differ from the reference program's by a relative error of at most 0.000065.
Values sent between devices are 32-bit elements; how exact they have to be, the bound alone decides.
No kernel may reach another device: no remote copies, remote signals or barrier semaphores. Data moves between devices by JAX's collectives and lax.ppermute only.
A program may use at most 320 MiB of HBM per device.

```python
import jax
import jax.numpy as jnp
from jax import lax

W = 256
NT = 96
O = 384
NOCC = 32
NVIR = 1600
P_SIZE = 24576


def draw_integrals(key, part):
    base_key = jax.random.fold_in(key, 11)
    key_one = jax.random.fold_in(base_key, 0)
    sample = jax.random.normal(key_one, (NT * W, NT * W), jnp.float32)
    return (sample + sample.T) * 0.5 ** 0.5 * (NT * W) ** (-0.5)


def draw_tile_mask(key, part):
    base_key = jax.random.fold_in(key, 23)
    key_one, key_two = jax.random.split(base_key)
    levels = jax.random.randint(key_one, (NT,), 0, 4)
    random_ints = jax.random.randint(key_two, (NT, NT), 0, 8)
    symmetric = jnp.triu(random_ints) + jnp.triu(random_ints, 1).T
    positions = jnp.arange(NT)
    keep = (symmetric < 1 + levels[:, None] + levels[None, :]) | (positions[:, None] == positions[None, :])
    return keep.astype(jnp.int32)


def occ_pairs(key):
    base_key = jax.random.fold_in(key, 37)
    key_one, key_two, key_three = jax.random.split(base_key, 3)
    shuffle = jax.random.permutation(key_one, O).astype(jnp.int32)
    pair_count = O // 2
    first_occ = jax.random.randint(key_two, (pair_count,), 0, NOCC)
    second_occ = (first_occ + 1 + jax.random.randint(key_three, (pair_count,), 0, NOCC - 1)) % NOCC
    even_cols = shuffle[0::2]
    odd_cols = shuffle[1::2]
    zero_cols = jnp.zeros((O,), jnp.int32)
    partner = zero_cols.at[even_cols].set(odd_cols).at[odd_cols].set(even_cols)
    occ_first = zero_cols.at[even_cols].set(first_occ).at[odd_cols].set(second_occ)
    occ_second = zero_cols.at[even_cols].set(second_occ).at[odd_cols].set(first_occ)
    return (partner, jnp.stack([occ_first, occ_second]).astype(jnp.int32))


def draw_occ_index(key, part):
    return occ_pairs(key)[1]


def draw_partner(key, part):
    return occ_pairs(key)[0]


def plant(drawn, stream_key, smallest, top_value):
    dims = drawn.shape
    place = [jax.random.randint(jax.random.fold_in(stream_key, axis), (), 0, dims[axis]) for axis in range(len(dims))]
    drawn = drawn.at[tuple(place)].set(smallest)
    longest = dims.index(max(dims))
    place[longest] = (place[longest] + 1) % dims[longest]
    return drawn.at[tuple(place)].set(top_value)


def steps_of(rng, dims, shards, least, largest):
    level = 1.0
    for axis_at, shards_of in shards:
        steps = jax.random.uniform(jax.random.fold_in(jax.random.fold_in(rng, 6), axis_at), (shards_of,), jnp.float32, least / len(shards), largest / len(shards))
        level = level * jnp.repeat(jnp.exp(steps), dims[axis_at] // shards_of).reshape((-1,) + (1,) * (len(dims) - 1 - axis_at))
    return level


def bell_draw(stream_key, shape, scale, most, pieces=(), held_as=jnp.bfloat16):
    entries = jax.random.normal(stream_key, shape, jnp.float32) * scale
    if len(pieces) > 0:
        entries = steps_of(stream_key, shape, pieces, -0.22, 0.18) * entries
    return jnp.clip(entries, min=-most, max=most).astype(held_as)


def setup_inputs(seed: int = 0) -> dict:
    splits = jax.random.split(jax.random.key(seed), 11)
    integrals = draw_integrals(jax.random.fold_in(splits[10], 71), 0)
    tile_mask = draw_tile_mask(jax.random.fold_in(splits[10], 71), 0)
    amplitudes = bell_draw(splits[2], (P_SIZE, O), 0.5, 4.0, ((0, 32),), jnp.float32)
    other_first = bell_draw(splits[3], (P_SIZE, O), 1.0, 6.0, ((0, 32),), jnp.float32)
    other_second = bell_draw(splits[4], (P_SIZE, O), 1.0, 6.0, ((0, 32),), jnp.float32)
    vir_index = plant(jax.random.randint(splits[5], (2, P_SIZE), 0, NVIR), jax.random.fold_in(splits[5], 1), 0, NVIR - 1).astype(jnp.int32)
    occ_index = draw_occ_index(jax.random.fold_in(splits[10], 71), 0)
    partner = draw_partner(jax.random.fold_in(splits[10], 71), 0)
    eps_vir = jnp.clip(jax.random.uniform(splits[8], (NVIR,), jnp.float32, 0.2, 3.0), 0.2, 3.0)
    eps_occ = jnp.clip(jax.random.uniform(splits[9], (NOCC,), jnp.float32, -2.0, -0.2), -2.0, -0.2)
    return {"integrals": integrals, "tile_mask": tile_mask, "amplitudes": amplitudes, "other_first": other_first, "other_second": other_second, "vir_index": vir_index, "occ_index": occ_index, "partner": partner, "eps_vir": eps_vir, "eps_occ": eps_occ}


precise = lax.Precision.HIGHEST


def ladder_sum(integrals, tile_mask, amplitude):
    def one_tile_row(tile_row):
        rows_part = lax.dynamic_slice_in_dim(integrals, tile_row * W, W, 0)
        weights = jnp.repeat(tile_mask[tile_row].astype(jnp.float32), W)
        return jnp.dot(rows_part * weights[None, :], amplitude, precision=precise, preferred_element_type=jnp.float32)

    stacked = lax.map(one_tile_row, jnp.arange(NT, dtype=jnp.int32))
    return stacked.reshape(NT * W, amplitude.shape[1])


def renew(ladder, other, denominator, partner):
    unscaled = (other + ladder) / denominator
    return 0.5 * (unscaled - jnp.take(unscaled, partner, axis=1))


def reference(integrals, tile_mask, amplitudes, other_first, other_second, vir_index, occ_index, partner, eps_vir, eps_occ):
    vir_energy = eps_vir[vir_index[0]] + eps_vir[vir_index[1]]
    occ_energy = eps_occ[occ_index[0]] + eps_occ[occ_index[1]]
    denominator = vir_energy[:, None] - occ_energy[None, :]
    first_update = renew(ladder_sum(integrals, tile_mask, amplitudes), other_first, denominator, partner)
    second_update = renew(ladder_sum(integrals, tile_mask, first_update), other_second, denominator, partner)
    return first_update, second_update
```

```python
import functools

import jax
import jax.numpy as jnp
from jax import lax
from jax.experimental import pallas as pl
from jax.experimental.pallas import tpu as pltpu
from jax.sharding import PartitionSpec as P

W = 256
GROUPS = 1
DEPTH = 12
UNROLL = 4


f32 = jnp.float32
bf16 = jnp.bfloat16
precise = lax.Precision.HIGHEST


def pair_energy(pair_index, table):
    orbitals = lax.broadcasted_iota(jnp.int32, (1, table.shape[0]), 1)
    counts = (pair_index[0][:, None] == orbitals).astype(f32) + (pair_index[1][:, None] == orbitals).astype(f32)
    return jnp.dot(counts, table, precision=precise, preferred_element_type=f32)


def renew(ladder, other, vir_rows, occ_energy, swap_matrix):
    unscaled = (other + ladder) / (vir_rows[:, None] - occ_energy[None, :])
    swapped = jnp.dot(unscaled, swap_matrix, precision=precise, preferred_element_type=f32)
    return 0.5 * (unscaled - swapped)


def general(
    integrals, tile_mask, amplitudes, other_first, other_second, vir_index, occ_index, partner, eps_vir, eps_occ
):
    row_count, col_count = integrals.shape
    tiles_down, tiles_across = tile_mask.shape
    weights = tile_mask.astype(f32)
    screened = (integrals.reshape(tiles_down, W, tiles_across, W) * weights[:, None, :, None]).reshape(
        row_count, col_count
    )
    occ_energy = pair_energy(occ_index, eps_occ)
    occ_cols = amplitudes.shape[1]
    column_ids = lax.broadcasted_iota(jnp.int32, (occ_cols, occ_cols), 0)
    swap_matrix = (column_ids == partner[None, :]).astype(f32)
    n_con = lax.axis_size("con")
    n_res = lax.axis_size("res")
    con_at = lax.axis_index("con")
    res_at = lax.axis_index("res")
    fine_rows = amplitudes.shape[0]

    def vir_rows(offset):
        return pair_energy(lax.dynamic_slice_in_dim(vir_index, offset, fine_rows, 1), eps_vir)

    partial_one = jnp.dot(
        screened,
        lax.all_gather(amplitudes, "res", axis=0, tiled=True),
        precision=precise,
        preferred_element_type=f32,
    )
    ladder_one = lax.psum_scatter(partial_one, "con", scatter_dimension=0, tiled=True)
    first_vir = vir_rows((res_at * n_con + con_at) * fine_rows)
    first_update = renew(ladder_one, other_first, first_vir, occ_energy, swap_matrix)
    partial_two = lax.dot_general(
        screened,
        lax.all_gather(first_update, "con", axis=0, tiled=True),
        (((0,), (0,)), ((), ())),
        precision=precise,
        preferred_element_type=f32,
    )
    ladder_two = lax.psum_scatter(partial_two, "res", scatter_dimension=0, tiled=True)
    second_vir = vir_rows((con_at * n_res + res_at) * fine_rows)
    second_update = renew(ladder_two, other_second, second_vir, occ_energy, swap_matrix)
    return (first_update, second_update)


def halves(value):
    high = value.astype(bf16)
    return high, (value - high.astype(f32)).astype(bf16)


def sweep_kernel(by_rows, n_in, has_start, bounds, row_of, col_of, strip_of, place_of, a_hbm, *refs):
    x_refs = refs[:n_in]
    start_ref = refs[n_in] if has_start else None
    y_ref, x_split, tiles, sems = refs[n_in + has_start :]
    width = x_refs[0].shape[0]
    at = 0
    for x_ref in x_refs:
        for j in range(x_ref.shape[1] // W):
            high, low = halves(x_ref[:, j * W : (j + 1) * W])
            x_split[at, :width, :] = high
            x_split[at, width:, :] = low
            at += 1
    y_ref[...] = start_ref[...] if has_start else jnp.zeros_like(y_ref)
    first = bounds[0]
    strip_base = bounds[2]
    count = bounds[1] - first

    def fetch(i):
        entry = first + i
        rows = pl.ds(pl.multiple_of(row_of[entry] * W, W), W)
        cols = pl.ds(pl.multiple_of(col_of[entry] * W, W), W)
        slot = lax.rem(i, DEPTH)
        return pltpu.make_async_copy(a_hbm.at[rows, cols], tiles.at[slot], sems.at[slot])

    for i in range(DEPTH):

        @pl.when(i < count)
        def _():
            fetch(i).start()

    def product(i):
        entry = first + i
        high, low = halves(tiles[lax.rem(i, DEPTH)])
        strip = strip_of[entry] - strip_base
        place = place_of[entry]
        source, target = (strip, place) if by_rows else (place, strip)
        dims = (((1,), (1 if by_rows else 0,)), ((), ()))
        both = x_split[source]
        main = lax.dot_general(both, high, dims, preferred_element_type=f32)
        rest = lax.dot_general(both[:width], low, dims, preferred_element_type=f32)
        return (main[:width] + main[width:]) + rest, pl.ds(pl.multiple_of(target * W, W), W)

    def several(block, _):
        at = block * UNROLL
        for u in range(UNROLL):
            fetch(at + u).wait()
        done = [product(at + u) for u in range(UNROLL)]
        for value, where in done:
            y_ref[:, where] += value
        for u in range(UNROLL):

            @pl.when(at + u + DEPTH < count)
            def _():
                fetch(at + u + DEPTH).start()

        return 0

    def single(i, _):
        fetch(i).wait()
        value, where = product(i)
        y_ref[:, where] += value
        return 0

    blocks = count // UNROLL
    lax.fori_loop(0, blocks, several, 0)
    lax.fori_loop(blocks * UNROLL, count, single, 0)


def sweep(by_rows, tables, bounds, integrals, x_list, y_width, start=None):
    width = x_list[0].shape[0]
    strips = sum(x.shape[1] for x in x_list) // W
    scalar = pl.BlockSpec(memory_space=pltpu.SMEM)
    vector = pl.BlockSpec(memory_space=pltpu.VMEM)
    has_start = start is not None
    inputs = list(x_list) + ([start] if has_start else [])
    tile_guess = integrals.shape[0] // W * 3
    return pl.pallas_call(
        functools.partial(sweep_kernel, by_rows, len(x_list), has_start),
        out_shape=jax.ShapeDtypeStruct((width, y_width), f32),
        in_specs=[scalar] * 5 + [pl.BlockSpec(memory_space=pl.ANY)] + [vector] * len(inputs),
        out_specs=vector,
        scratch_shapes=[
            pltpu.VMEM((strips, 2 * width, W), bf16),
            pltpu.VMEM((DEPTH, W, W), f32),
            pltpu.SemaphoreType.DMA((DEPTH,)),
        ],
        input_output_aliases={5 + len(inputs): 0} if has_start else {},
        compiler_params=pltpu.CompilerParams(vmem_limit_bytes=32 * 2**20),
        cost_estimate=pl.CostEstimate(
            flops=6 * width * W * W * tile_guess, bytes_accessed=4 * W * W * tile_guess, transcendentals=0
        ),
        name="rows_sweep" if by_rows else "cols_sweep",
    )(bounds, *tables, integrals, *inputs)


def ring_order(n):
    return list(range(0, n, 2)) + list(range(n - 1, 0, -2))


def bit_reverse(value, bits):
    out = jnp.zeros_like(value)
    for b in range(bits):
        out = out + ((value >> b) & 1) * (1 << (bits - 1 - b))
    return out


def tile_tables(tile_mask, order, res_at, con_at, n_con, strip_tiles):
    down, across = tile_mask.shape
    n = len(order)
    ring = jnp.array(order, jnp.int32)
    my_place = jnp.sum(jnp.where(ring == res_at, jnp.arange(n, dtype=jnp.int32), 0))
    steps = [0]
    for s in range(1, n // 2):
        steps += [-s, s]
    steps.append(n // 2)
    places = lax.rem(my_place + jnp.array(steps, jnp.int32) + n, n)
    owners = jnp.sum(jnp.where(places[:, None] == jnp.arange(n, dtype=jnp.int32)[None, :], ring[None, :], 0), axis=1)
    cols = (owners[:, None] * strip_tiles + jnp.arange(strip_tiles, dtype=jnp.int32)[None, :]).reshape(across)
    chosen = (cols[:, None] == jnp.arange(across, dtype=jnp.int32)[None, :]).astype(f32)
    kept = lax.dot_general(chosen, (tile_mask != 0).astype(f32), (((1,), (1,)), ((), ())), preferred_element_type=f32)
    flags = kept.reshape(across * down).astype(jnp.int32)
    total = across * down
    entry = jnp.arange(total, dtype=jnp.int32)
    before = jnp.sum(jnp.where(entry[None, :] < entry[:, None], flags[None, :], 0), axis=1)
    slot = jnp.where(flags > 0, before, total)
    listed = jnp.sum(jnp.where(slot[None, :] == entry[:, None], entry[None, :], 0), axis=1)
    strip = listed // down
    row = listed - strip * down
    col = jnp.sum(jnp.where(strip[:, None] == jnp.arange(across, dtype=jnp.int32)[None, :], cols[None, :], 0), axis=1)
    bits = n_con.bit_length() - 1
    piece = row // strip_tiles
    place = bit_reverse(piece ^ con_at, bits) * strip_tiles + (row - piece * strip_tiles)
    edges = jnp.arange(n + 1, dtype=jnp.int32) * (strip_tiles * down)
    starts = jnp.sum(jnp.where(entry[None, :] < edges[:, None], flags[None, :], 0), axis=1)
    return (row, col, strip, place), starts


def vir_energies(vir_index, eps_vir, offset, count):
    picked = lax.dynamic_slice_in_dim(vir_index, offset, count, 1)
    orbitals = lax.broadcasted_iota(jnp.int32, (eps_vir.shape[0], 1), 0)
    table = eps_vir[:, None]
    first = jnp.sum(jnp.where(picked[0][None, :] == orbitals, table, 0.0), axis=0)
    second = jnp.sum(jnp.where(picked[1][None, :] == orbitals, table, 0.0), axis=0)
    return first + second


def tiled(
    integrals, tile_mask, amplitudes, other_first, other_second, vir_index, occ_index, partner, eps_vir, eps_occ
):
    n_con = lax.axis_size("con")
    n_res = lax.axis_size("res")
    con_at = lax.axis_index("con")
    res_at = lax.axis_index("res")
    fine, occ_cols = amplitudes.shape
    rows, cols = integrals.shape
    strip_tiles = fine // W
    pairs = occ_cols // 2
    width = pairs // GROUPS

    column = jnp.arange(occ_cols, dtype=jnp.int32)
    lead = column < partner
    low = jnp.minimum(column, partner)
    pair_of = jnp.sum(jnp.where(column[None, :] < low[:, None], lead[None, :].astype(jnp.int32), 0), axis=1)
    is_pair = jnp.arange(pairs, dtype=jnp.int32)[:, None] == pair_of[None, :]
    chosen = (is_pair & lead[None, :]).astype(f32)
    signed = jnp.where(is_pair, jnp.where(lead, 1.0, -1.0)[None, :], 0.0).astype(f32)

    def compact(value):
        return lax.dot_general(
            signed, value, (((1,), (1,)), ((), ())), precision=precise, preferred_element_type=f32
        )

    def expand(value):
        return lax.dot_general(
            value, signed, (((0,), (0,)), ((), ())), precision=precise, preferred_element_type=f32
        )

    occ_orbitals = lax.broadcasted_iota(jnp.int32, (eps_occ.shape[0], 1), 0)
    occ_energy = jnp.sum(jnp.where(occ_index[0][None, :] == occ_orbitals, eps_occ[:, None], 0.0), axis=0) + jnp.sum(
        jnp.where(occ_index[1][None, :] == occ_orbitals, eps_occ[:, None], 0.0), axis=0
    )
    occ_pair = jnp.sum(chosen * occ_energy[None, :], axis=1)
    first_vir = vir_energies(vir_index, eps_vir, (res_at * n_con + con_at) * fine, fine)
    second_vir = vir_energies(vir_index, eps_vir, (con_at * n_res + res_at) * fine, fine)
    first_scale = first_vir[None, :] - occ_pair[:, None]
    second_scale = second_vir[None, :] - occ_pair[:, None]

    order = ring_order(n_res)
    onward = [(order[i], order[(i + 1) % n_res]) for i in range(n_res)]
    backward = [(b, a) for a, b in onward]
    tables, starts = tile_tables(tile_mask, order, res_at, con_at, n_con, strip_tiles)

    def bounds(j, k):
        return jnp.stack([starts[j], starts[k], jnp.int32(j * strip_tiles)])

    def part(value, g):
        return value[g * width : (g + 1) * width]

    x_all = compact(amplitudes)
    first_other = compact(other_first)
    second_other = compact(other_second)
    firsts, seconds = [], []
    half = width // 2
    for g in range(GROUPS):
        own = part(x_all, g)
        ahead = behind = own
        ladder = sweep(True, tables, bounds(0, 1), integrals, [own], rows)
        for s in range(1, n_res // 2):
            ahead, behind = lax.ppermute(ahead, "res", onward), lax.ppermute(behind, "res", backward)
            ladder = sweep(True, tables, bounds(2 * s - 1, 2 * s + 1), integrals, [ahead, behind], rows, ladder)
        far = jnp.concatenate(
            [lax.ppermute(ahead[:half], "res", onward), lax.ppermute(behind[half:], "res", backward)], axis=0
        )
        ladder = sweep(True, tables, bounds(n_res - 1, n_res), integrals, [far], rows, ladder)
        bit = 1
        while bit < n_con:
            swap = [(i, i ^ bit) for i in range(n_con)]
            mid = ladder.shape[1] // 2
            ladder = ladder[:, :mid] + lax.ppermute(ladder[:, mid:], "con", swap)
            bit *= 2
        first = 0.5 * (part(first_other, g) + ladder) / part(first_scale, g)
        firsts.append(first)
        held = [first]
        while bit > 1:
            bit //= 2
            swap = [(i, i ^ bit) for i in range(n_con)]
            block = jnp.concatenate(held, axis=1) if len(held) > 1 else held[0]
            held = held + [lax.ppermute(block, "con", swap)]
        far = sweep(False, tables, bounds(n_res - 1, n_res), integrals, held, fine)
        ahead = lax.ppermute(far[:half], "res", onward)
        behind = lax.ppermute(far[half:], "res", backward)
        for s in range(n_res // 2 - 1, 0, -1):
            both = sweep(False, tables, bounds(2 * s - 1, 2 * s + 1), integrals, held, 2 * fine)
            to_behind, to_ahead = both[:, :fine], both[:, fine:]
            if s == n_res // 2 - 1:
                to_ahead = jnp.concatenate([to_ahead[:half] + ahead, to_ahead[half:]], axis=0)
                to_behind = jnp.concatenate([to_behind[:half], to_behind[half:] + behind], axis=0)
            else:
                to_ahead, to_behind = to_ahead + ahead, to_behind + behind
            ahead = lax.ppermute(to_ahead, "res", onward)
            behind = lax.ppermute(to_behind, "res", backward)
        mine = sweep(False, tables, bounds(0, 1), integrals, held, fine)
        ladder = mine + ahead + behind
        seconds.append((0.5 * part(second_other, g) + ladder) / part(second_scale, g))
    first = jnp.concatenate(firsts, axis=0) if GROUPS > 1 else firsts[0]
    second = jnp.concatenate(seconds, axis=0) if GROUPS > 1 else seconds[0]
    return expand(first), expand(second)


def per_device(integrals, tile_mask, amplitudes, *rest):
    n_con = lax.axis_size("con")
    n_res = lax.axis_size("res")
    fits = (
        amplitudes.shape[0] % W == 0
        and amplitudes.shape[1] % (16 * GROUPS) == 0
        and n_con & (n_con - 1) == 0
        and n_res % 2 == 0
        and n_res > 2
    )
    return (tiled if fits else general)(integrals, tile_mask, amplitudes, *rest)


def solution(mesh):
    return jax.shard_map(
        per_device,
        mesh=mesh,
        in_specs=(
            P("res", "con"),
            P("res", "con"),
            P(("con", "res"), None),
            P(("res", "con"), None),
            P(("con", "res"), None),
            P(),
            P(),
            P(),
            P(),
            P(),
        ),
        out_specs=(P(("res", "con"), None), P(("con", "res"), None)),
        check_vma=False,
    )
```

```python
import functools

import jax
import jax.numpy as jnp
from jax import lax
from jax.experimental import pallas as pl
from jax.experimental.pallas import tpu as pltpu
from jax.sharding import PartitionSpec as P


W = 256
PARTS = 2
DEPTH = 12
UNROLL = 4


f32 = jnp.float32
bf16 = jnp.bfloat16
precise = lax.Precision.HIGHEST


def pair_energy(pair_index, table):
    orbitals = lax.broadcasted_iota(jnp.int32, (1, table.shape[0]), 1)
    counts = (pair_index[0][:, None] == orbitals).astype(f32) + (pair_index[1][:, None] == orbitals).astype(f32)
    return jnp.dot(counts, table, precision=precise, preferred_element_type=f32)


def renew(ladder, other, vir_rows, occ_energy, swap_matrix):
    unscaled = (other + ladder) / (vir_rows[:, None] - occ_energy[None, :])
    swapped = jnp.dot(unscaled, swap_matrix, precision=precise, preferred_element_type=f32)
    return 0.5 * (unscaled - swapped)


def general(
    integrals, tile_mask, amplitudes, other_first, other_second, vir_index, occ_index, partner, eps_vir, eps_occ
):
    row_count, col_count = integrals.shape
    tiles_down, tiles_across = tile_mask.shape
    weights = tile_mask.astype(f32)
    screened = (integrals.reshape(tiles_down, W, tiles_across, W) * weights[:, None, :, None]).reshape(
        row_count, col_count
    )
    occ_energy = pair_energy(occ_index, eps_occ)
    occ_cols = amplitudes.shape[1]
    column_ids = lax.broadcasted_iota(jnp.int32, (occ_cols, occ_cols), 0)
    swap_matrix = (column_ids == partner[None, :]).astype(f32)
    n_con = lax.axis_size("con")
    n_res = lax.axis_size("res")
    con_at = lax.axis_index("con")
    res_at = lax.axis_index("res")
    fine_rows = amplitudes.shape[0]

    def vir_rows(offset):
        return pair_energy(lax.dynamic_slice_in_dim(vir_index, offset, fine_rows, 1), eps_vir)

    partial_one = jnp.dot(
        screened,
        lax.all_gather(amplitudes, "res", axis=0, tiled=True),
        precision=precise,
        preferred_element_type=f32,
    )
    ladder_one = lax.psum_scatter(partial_one, "con", scatter_dimension=0, tiled=True)
    first_vir = vir_rows((res_at * n_con + con_at) * fine_rows)
    first_update = renew(ladder_one, other_first, first_vir, occ_energy, swap_matrix)
    partial_two = lax.dot_general(
        screened,
        lax.all_gather(first_update, "con", axis=0, tiled=True),
        (((0,), (0,)), ((), ())),
        precision=precise,
        preferred_element_type=f32,
    )
    ladder_two = lax.psum_scatter(partial_two, "res", scatter_dimension=0, tiled=True)
    second_vir = vir_rows((con_at * n_res + res_at) * fine_rows)
    second_update = renew(ladder_two, other_second, second_vir, occ_energy, swap_matrix)
    return (first_update, second_update)


def halves(value):
    high = value.astype(bf16)
    return high, (value - high.astype(f32)).astype(bf16)


def sweep_kernel(by_rows, blocks, n_parts, has_start, n_out, strip_base, edge, starts, row_of, col_of, strip_of, place_of, a_hbm, *refs):
    n_x = len(blocks) * n_parts
    x_refs = refs[:n_x]
    start_ref = refs[n_x] if has_start else None
    refs = refs[n_x + has_start :]
    out_refs, refs = refs[:n_out], refs[n_out:]
    y_ref = out_refs[0] if n_out == 1 else refs[0]
    refs = refs if n_out == 1 else refs[1:]
    x_split, tiles, sems, x_sem = refs[:4]
    x_whole = refs[4:]
    first = starts[edge[0]]
    count = starts[edge[1]] - first

    def fetch(i):
        entry = first + i
        rows = pl.ds(pl.multiple_of(row_of[entry] * W, W), W)
        cols = pl.ds(pl.multiple_of(col_of[entry] * W, W), W)
        slot = lax.rem(i, DEPTH)
        return pltpu.make_async_copy(a_hbm.at[rows, cols], tiles.at[slot], sems.at[slot])

    part_rows = y_ref.shape[0] // n_parts
    loads = []
    for n in range(n_x):
        part = pl.ds((n % n_parts) * part_rows, part_rows)
        loads.append(pltpu.make_async_copy(x_refs[n], x_whole[n // n_parts].at[part, :], x_sem.at[n]))
        loads[-1].start()
    for i in range(DEPTH):

        @pl.when(i < count)
        def _():
            fetch(i).start()

    y_ref[...] = start_ref[...] if has_start else jnp.zeros_like(y_ref)
    width = y_ref.shape[0]
    at = 0
    for n in range(len(blocks)):
        for p in range(n_parts):
            loads[n * n_parts + p].wait()
        for j in range(blocks[n] // W):
            high, low = halves(x_whole[n][:, j * W : (j + 1) * W])
            x_split[at, :width, :] = high
            x_split[at, width:, :] = low
            at += 1

    def product(i):
        entry = first + i
        high, low = halves(tiles[lax.rem(i, DEPTH)])
        strip = strip_of[entry] - strip_base
        place = place_of[entry]
        source, target = (strip, place) if by_rows else (place, strip)
        dims = (((1,), (1 if by_rows else 0,)), ((), ()))
        both = x_split[source]
        main = lax.dot_general(both, high, dims, preferred_element_type=f32)
        rest = lax.dot_general(both[:width], low, dims, preferred_element_type=f32)
        return (main[:width] + main[width:]) + rest, pl.ds(pl.multiple_of(target * W, W), W)

    def several(block, _):
        at = block * UNROLL
        for u in range(UNROLL):
            fetch(at + u).wait()
        done = [product(at + u) for u in range(UNROLL)]
        for value, where in done:
            y_ref[:, where] += value
        for u in range(UNROLL):

            @pl.when(at + u + DEPTH < count)
            def _():
                fetch(at + u + DEPTH).start()

        return 0

    def single(i, _):
        fetch(i).wait()
        value, where = product(i)
        y_ref[:, where] += value
        return 0

    several_of = count // UNROLL
    lax.fori_loop(0, several_of, several, 0)
    lax.fori_loop(several_of * UNROLL, count, single, 0)
    if n_out > 1:
        out_cols = out_refs[0].shape[1]
        for n, out_ref in enumerate(out_refs):
            p, c = n % n_parts, n // n_parts
            out_ref[...] = y_ref[p * part_rows : (p + 1) * part_rows, c * out_cols : (c + 1) * out_cols]


def sweep(by_rows, tables, starts, edge, strip_tiles, integrals, x_blocks, y_width, start=None, pieces=0):
    n_parts = len(x_blocks[0])
    part_rows = x_blocks[0][0].shape[0]
    width = n_parts * part_rows
    blocks = [block[0].shape[1] for block in x_blocks]
    inputs = [part for block in x_blocks for part in block]
    scalar = pl.BlockSpec(memory_space=pltpu.SMEM)
    vector = pl.BlockSpec(memory_space=pltpu.VMEM)
    anywhere = pl.BlockSpec(memory_space=pl.ANY)
    has_start = start is not None
    n_out = pieces * n_parts if pieces else 1
    whole = jax.ShapeDtypeStruct((width, y_width), f32)
    tile_guess = (edge[1] - edge[0]) * strip_tiles * (integrals.shape[0] // W) // 2
    extra = [pltpu.VMEM((width, y_width), f32)] if pieces else []
    return pl.pallas_call(
        functools.partial(
            sweep_kernel, by_rows, blocks, n_parts, int(has_start), n_out, edge[0] * strip_tiles, edge
        ),
        out_shape=[jax.ShapeDtypeStruct((part_rows, y_width // pieces), f32)] * n_out if pieces else whole,
        in_specs=[scalar] * 5 + [anywhere] * (1 + len(inputs)) + [vector] * has_start,
        out_specs=[vector] * n_out if pieces else vector,
        scratch_shapes=extra
        + [
            pltpu.VMEM((sum(blocks) // W, 2 * width, W), bf16),
            pltpu.VMEM((DEPTH, W, W), f32),
            pltpu.SemaphoreType.DMA((DEPTH,)),
            pltpu.SemaphoreType.DMA((len(inputs),)),
        ]
        + [pltpu.VMEM((width, n), f32) for n in blocks],
        input_output_aliases={6 + len(inputs): 0} if has_start and not pieces else {},
        compiler_params=pltpu.CompilerParams(vmem_limit_bytes=32 * 2**20),
        cost_estimate=pl.CostEstimate(
            flops=6 * width * W * W * tile_guess, bytes_accessed=4 * W * W * tile_guess, transcendentals=0
        ),
        name="rows_sweep" if by_rows else "cols_sweep",
    )(starts, *tables, integrals, *inputs, *([start] if has_start else []))


def ring_order(n):
    return list(range(0, n, 2)) + list(range(n - 1, 0, -2))


def bit_reverse(value, bits):
    out = jnp.zeros_like(value)
    for b in range(bits):
        out = out + ((value >> b) & 1) * (1 << (bits - 1 - b))
    return out


def tile_tables(tile_mask, order, res_at, con_at, n_con, strip_tiles):
    down, across = tile_mask.shape
    n = len(order)
    ring = jnp.array(order, jnp.int32)
    my_place = jnp.sum(jnp.where(ring == res_at, jnp.arange(n, dtype=jnp.int32), 0))
    steps = [0]
    for s in range(1, n // 2):
        steps += [-s, s]
    steps.append(n // 2)
    places = lax.rem(my_place + jnp.array(steps, jnp.int32) + n, n)
    owners = jnp.sum(jnp.where(places[:, None] == jnp.arange(n, dtype=jnp.int32)[None, :], ring[None, :], 0), axis=1)
    cols = (owners[:, None] * strip_tiles + jnp.arange(strip_tiles, dtype=jnp.int32)[None, :]).reshape(across)
    chosen = (cols[:, None] == jnp.arange(across, dtype=jnp.int32)[None, :]).astype(f32)
    kept = lax.dot_general(chosen, (tile_mask != 0).astype(f32), (((1,), (1,)), ((), ())), preferred_element_type=f32)
    flags = kept.reshape(across * down).astype(jnp.int32)
    total = across * down
    entry = jnp.arange(total, dtype=jnp.int32)
    before = jnp.sum(jnp.where(entry[None, :] < entry[:, None], flags[None, :], 0), axis=1)
    slot = jnp.where(flags > 0, before, total)
    listed = jnp.sum(jnp.where(slot[None, :] == entry[:, None], entry[None, :], 0), axis=1)
    strip = listed // down
    row = listed - strip * down
    col = jnp.sum(jnp.where(strip[:, None] == jnp.arange(across, dtype=jnp.int32)[None, :], cols[None, :], 0), axis=1)
    bits = n_con.bit_length() - 1
    piece = row // strip_tiles
    place = bit_reverse(piece ^ con_at, bits) * strip_tiles + (row - piece * strip_tiles)
    edges = jnp.arange(n + 1, dtype=jnp.int32) * (strip_tiles * down)
    starts = jnp.sum(jnp.where(entry[None, :] < edges[:, None], flags[None, :], 0), axis=1)
    return (row, col, strip, place), starts


def vir_energies(vir_index, eps_vir, offset, count):
    picked = lax.dynamic_slice_in_dim(vir_index, offset, count, 1)
    orbitals = lax.broadcasted_iota(jnp.int32, (eps_vir.shape[0], 1), 0)
    table = eps_vir[:, None]
    first = jnp.sum(jnp.where(picked[0][None, :] == orbitals, table, 0.0), axis=0)
    second = jnp.sum(jnp.where(picked[1][None, :] == orbitals, table, 0.0), axis=0)
    return first + second


def tiled(
    integrals, tile_mask, amplitudes, other_first, other_second, vir_index, occ_index, partner, eps_vir, eps_occ
):
    n_con = lax.axis_size("con")
    n_res = lax.axis_size("res")
    con_at = lax.axis_index("con")
    res_at = lax.axis_index("res")
    fine, occ_cols = amplitudes.shape
    rows, _ = integrals.shape
    strip_tiles = fine // W
    pairs = occ_cols // 2
    width = pairs // PARTS
    parts = range(PARTS)

    column = jnp.arange(occ_cols, dtype=jnp.int32)
    lead = column < partner
    low = jnp.minimum(column, partner)
    pair_of = jnp.sum(jnp.where(column[None, :] < low[:, None], lead[None, :].astype(jnp.int32), 0), axis=1)
    is_pair = jnp.arange(pairs, dtype=jnp.int32)[:, None] == pair_of[None, :]
    chosen = (is_pair & lead[None, :]).astype(f32)
    signed = jnp.where(is_pair, jnp.where(lead, 1.0, -1.0)[None, :], 0.0).astype(f32)

    def compact(value):
        return lax.dot_general(
            signed, value, (((1,), (1,)), ((), ())), precision=precise, preferred_element_type=f32
        )

    def expand(value):
        return lax.dot_general(
            value, signed, (((0,), (0,)), ((), ())), precision=precise, preferred_element_type=f32
        )

    occ_orbitals = lax.broadcasted_iota(jnp.int32, (eps_occ.shape[0], 1), 0)
    occ_energy = jnp.sum(jnp.where(occ_index[0][None, :] == occ_orbitals, eps_occ[:, None], 0.0), axis=0) + jnp.sum(
        jnp.where(occ_index[1][None, :] == occ_orbitals, eps_occ[:, None], 0.0), axis=0
    )
    occ_pair = jnp.sum(chosen * occ_energy[None, :], axis=1)
    order = ring_order(n_res)
    onward = [(order[i], order[(i + 1) % n_res]) for i in range(n_res)]
    backward = [(b, a) for a, b in onward]
    tables, starts = tile_tables(tile_mask, order, res_at, con_at, n_con, strip_tiles)
    rows_sweep = functools.partial(sweep, True, tables, starts)
    cols_sweep = functools.partial(sweep, False, tables, starts)

    def cut(value):
        return [value[p * width : (p + 1) * width] for p in parts]

    def send(values, axis, perm):
        return [lax.ppermute(value, axis, perm) for value in values]

    def scales(index, offset):
        return cut(vir_energies(index, eps_vir, offset, fine)[None, :] - occ_pair[:, None])

    near = n_res // 2
    own = cut(compact(amplitudes))
    ahead = behind = own
    blocks = [own]
    ladder = None
    for s in range(1, near):
        ahead, behind = send(ahead, "res", onward), send(behind, "res", backward)
        blocks += [ahead, behind]
        edge = (2 * s + 1 - len(blocks), 2 * s + 1)
        ladder = rows_sweep(edge, strip_tiles, integrals, blocks, rows, ladder)
        blocks = []
    far = send(ahead[: PARTS // 2], "res", onward) + send(behind[PARTS // 2 :], "res", backward)
    pieces = rows_sweep((n_res - 1, n_res), strip_tiles, integrals, [far], rows, ladder, pieces=2)
    kept, sent = pieces[:PARTS], pieces[PARTS:]
    first_other = compact(other_first)
    bit = 1
    while bit < n_con:
        swap = [(i, i ^ bit) for i in range(n_con)]
        came = send(sent, "con", swap)
        bit *= 2
        if bit < n_con:
            mid = kept[0].shape[1] // 2
            sent = [kept[p][:, mid:] + came[p][:, mid:] for p in parts]
            kept = [kept[p][:, :mid] + came[p][:, :mid] for p in parts]
            late_index, sent[0] = lax.optimization_barrier((vir_index, sent[0]))
    first_scale = scales(late_index, (res_at * n_con + con_at) * fine)
    firsts = [0.5 * (part + (kept[p] + came[p])) / first_scale[p] for p, part in enumerate(cut(first_other))]
    held = [firsts]
    while bit > 1:
        bit //= 2
        swap = [(i, i ^ bit) for i in range(n_con)]
        block = [jnp.concatenate([h[p] for h in held], axis=1) if len(held) > 1 else held[0][p] for p in parts]
        held = held + [send(block, "con", swap)]
    far = cols_sweep((n_res - 1, n_res), strip_tiles, integrals, held, fine, pieces=1)
    ahead = [lax.ppermute(far[p], "res", onward) if p < PARTS // 2 else None for p in parts]
    behind = [None if p < PARTS // 2 else lax.ppermute(far[p], "res", backward) for p in parts]
    late_index, second_other_rows, _ = lax.optimization_barrier((vir_index, other_second, far[0]))
    for s in range(near - 1, 0, -1):
        edge = (2 * s - 1, 2 * s + 1)
        both = cols_sweep(edge, strip_tiles, integrals, held, 2 * fine, pieces=2)
        to_behind, to_ahead = both[:PARTS], both[PARTS:]
        ahead = send([to_ahead[p] if ahead[p] is None else to_ahead[p] + ahead[p] for p in parts], "res", onward)
        behind = send([to_behind[p] if behind[p] is None else to_behind[p] + behind[p] for p in parts], "res", backward)
    mine = cols_sweep((0, 1), strip_tiles, integrals, held, fine, pieces=1)
    second_other = cut(compact(second_other_rows))
    second_scale = scales(late_index, (con_at * n_res + res_at) * fine)
    seconds = [
        (0.5 * second_other[p] + ((mine[p] + ahead[p]) + behind[p])) / second_scale[p] for p in parts
    ]
    return expand(jnp.concatenate(firsts, axis=0)), expand(jnp.concatenate(seconds, axis=0))


def per_device(integrals, tile_mask, amplitudes, *rest):
    n_con = lax.axis_size("con")
    n_res = lax.axis_size("res")
    fits = (
        amplitudes.shape[0] % W == 0
        and amplitudes.shape[1] % (32 * PARTS) == 0
        and n_con & (n_con - 1) == 0
        and n_res % 2 == 0
        and n_res > 2
    )
    if not fits:
        return general(integrals, tile_mask, amplitudes, *rest)
    return tiled(integrals, tile_mask, amplitudes, *rest)


def solution(mesh):
    return jax.shard_map(
        per_device,
        mesh=mesh,
        in_specs=(
            P("res", "con"),
            P("res", "con"),
            P(("con", "res"), None),
            P(("res", "con"), None),
            P(("con", "res"), None),
            P(),
            P(),
            P(),
            P(),
            P(),
        ),
        out_specs=(P(("res", "con"), None), P(("con", "res"), None)),
        check_vma=False,
    )
```

```python
import functools

import jax
import jax.numpy as jnp
from jax import lax
from jax.experimental import pallas as pl
from jax.experimental.pallas import tpu as pltpu
from jax.sharding import PartitionSpec as P


W = 256
PARTS = 2
DEPTH = 12
UNROLL = 4


f32 = jnp.float32
bf16 = jnp.bfloat16
precise = lax.Precision.HIGHEST


def pair_energy(pair_index, table):
    orbitals = lax.broadcasted_iota(jnp.int32, (1, table.shape[0]), 1)
    counts = (pair_index[0][:, None] == orbitals).astype(f32) + (pair_index[1][:, None] == orbitals).astype(f32)
    return jnp.dot(counts, table, precision=precise, preferred_element_type=f32)


def renew(ladder, other, vir_rows, occ_energy, swap_matrix):
    unscaled = (other + ladder) / (vir_rows[:, None] - occ_energy[None, :])
    swapped = jnp.dot(unscaled, swap_matrix, precision=precise, preferred_element_type=f32)
    return 0.5 * (unscaled - swapped)


def general(
    integrals, tile_mask, amplitudes, other_first, other_second, vir_index, occ_index, partner, eps_vir, eps_occ
):
    row_count, col_count = integrals.shape
    tiles_down, tiles_across = tile_mask.shape
    weights = tile_mask.astype(f32)
    screened = (integrals.reshape(tiles_down, W, tiles_across, W) * weights[:, None, :, None]).reshape(
        row_count, col_count
    )
    occ_energy = pair_energy(occ_index, eps_occ)
    occ_cols = amplitudes.shape[1]
    column_ids = lax.broadcasted_iota(jnp.int32, (occ_cols, occ_cols), 0)
    swap_matrix = (column_ids == partner[None, :]).astype(f32)
    n_con = lax.axis_size("con")
    n_res = lax.axis_size("res")
    con_at = lax.axis_index("con")
    res_at = lax.axis_index("res")
    fine_rows = amplitudes.shape[0]

    def vir_rows(offset):
        return pair_energy(lax.dynamic_slice_in_dim(vir_index, offset, fine_rows, 1), eps_vir)

    partial_one = jnp.dot(
        screened,
        lax.all_gather(amplitudes, "res", axis=0, tiled=True),
        precision=precise,
        preferred_element_type=f32,
    )
    ladder_one = lax.psum_scatter(partial_one, "con", scatter_dimension=0, tiled=True)
    first_vir = vir_rows((res_at * n_con + con_at) * fine_rows)
    first_update = renew(ladder_one, other_first, first_vir, occ_energy, swap_matrix)
    partial_two = lax.dot_general(
        screened,
        lax.all_gather(first_update, "con", axis=0, tiled=True),
        (((0,), (0,)), ((), ())),
        precision=precise,
        preferred_element_type=f32,
    )
    ladder_two = lax.psum_scatter(partial_two, "res", scatter_dimension=0, tiled=True)
    second_vir = vir_rows((con_at * n_res + res_at) * fine_rows)
    second_update = renew(ladder_two, other_second, second_vir, occ_energy, swap_matrix)
    return (first_update, second_update)


def halves(value):
    high = value.astype(bf16)
    return high, (value - high.astype(f32)).astype(bf16)


def sweep_kernel(by_rows, blocks, n_parts, has_start, n_out, strip_base, edge, starts, row_of, col_of, strip_of, place_of, a_hbm, *refs):
    n_x = len(blocks) * n_parts
    x_refs = refs[:n_x]
    start_ref = refs[n_x] if has_start else None
    refs = refs[n_x + has_start :]
    out_refs, refs = refs[:n_out], refs[n_out:]
    y_ref = out_refs[0] if n_out == 1 else refs[0]
    refs = refs if n_out == 1 else refs[1:]
    x_split, tiles, sems, x_sem = refs[:4]
    x_whole = refs[4:]
    first = starts[edge[0]]
    count = starts[edge[1]] - first

    def fetch(i):
        entry = first + i
        rows = pl.ds(pl.multiple_of(row_of[entry] * W, W), W)
        cols = pl.ds(pl.multiple_of(col_of[entry] * W, W), W)
        slot = lax.rem(i, DEPTH)
        return pltpu.make_async_copy(a_hbm.at[rows, cols], tiles.at[slot], sems.at[slot])

    part_rows = y_ref.shape[0] // n_parts
    loads = []
    for n in range(n_x):
        part = pl.ds((n % n_parts) * part_rows, part_rows)
        loads.append(pltpu.make_async_copy(x_refs[n], x_whole[n // n_parts].at[part, :], x_sem.at[n]))
        loads[-1].start()
    for i in range(DEPTH):

        @pl.when(i < count)
        def _():
            fetch(i).start()

    y_ref[...] = start_ref[...] if has_start else jnp.zeros_like(y_ref)
    width = y_ref.shape[0]
    at = 0
    for n in range(len(blocks)):
        for p in range(n_parts):
            loads[n * n_parts + p].wait()
        for j in range(blocks[n] // W):
            high, low = halves(x_whole[n][:, j * W : (j + 1) * W])
            x_split[at, :width, :] = high
            x_split[at, width:, :] = low
            at += 1

    def product(i):
        entry = first + i
        high, low = halves(tiles[lax.rem(i, DEPTH)])
        strip = strip_of[entry] - strip_base
        place = place_of[entry]
        source, target = (strip, place) if by_rows else (place, strip)
        dims = (((1,), (1 if by_rows else 0,)), ((), ()))
        both = x_split[source]
        main = lax.dot_general(both, high, dims, preferred_element_type=f32)
        rest = lax.dot_general(both[:width], low, dims, preferred_element_type=f32)
        return (main[:width] + main[width:]) + rest, pl.ds(pl.multiple_of(target * W, W), W)

    def several(block, _):
        at = block * UNROLL
        for u in range(UNROLL):
            fetch(at + u).wait()
        done = [product(at + u) for u in range(UNROLL)]
        for value, where in done:
            y_ref[:, where] += value
        for u in range(UNROLL):

            @pl.when(at + u + DEPTH < count)
            def _():
                fetch(at + u + DEPTH).start()

        return 0

    def single(i, _):
        fetch(i).wait()
        value, where = product(i)
        y_ref[:, where] += value
        return 0

    several_of = count // UNROLL
    lax.fori_loop(0, several_of, several, 0)
    lax.fori_loop(several_of * UNROLL, count, single, 0)
    if n_out > 1:
        out_cols = out_refs[0].shape[1]
        for n, out_ref in enumerate(out_refs):
            p, c = n % n_parts, n // n_parts
            out_ref[...] = y_ref[p * part_rows : (p + 1) * part_rows, c * out_cols : (c + 1) * out_cols]


def sweep(by_rows, tables, starts, edge, strip_tiles, integrals, x_blocks, y_width, start=None, pieces=0):
    n_parts = len(x_blocks[0])
    part_rows = x_blocks[0][0].shape[0]
    width = n_parts * part_rows
    blocks = [block[0].shape[1] for block in x_blocks]
    inputs = [part for block in x_blocks for part in block]
    scalar = pl.BlockSpec(memory_space=pltpu.SMEM)
    vector = pl.BlockSpec(memory_space=pltpu.VMEM)
    anywhere = pl.BlockSpec(memory_space=pl.ANY)
    has_start = start is not None
    n_out = pieces * n_parts if pieces else 1
    whole = jax.ShapeDtypeStruct((width, y_width), f32)
    tile_guess = (edge[1] - edge[0]) * strip_tiles * (integrals.shape[0] // W) // 2
    extra = [pltpu.VMEM((width, y_width), f32)] if pieces else []
    return pl.pallas_call(
        functools.partial(
            sweep_kernel, by_rows, blocks, n_parts, int(has_start), n_out, edge[0] * strip_tiles, edge
        ),
        out_shape=[jax.ShapeDtypeStruct((part_rows, y_width // pieces), f32)] * n_out if pieces else whole,
        in_specs=[scalar] * 5 + [anywhere] * (1 + len(inputs)) + [vector] * has_start,
        out_specs=[vector] * n_out if pieces else vector,
        scratch_shapes=extra
        + [
            pltpu.VMEM((sum(blocks) // W, 2 * width, W), bf16),
            pltpu.VMEM((DEPTH, W, W), f32),
            pltpu.SemaphoreType.DMA((DEPTH,)),
            pltpu.SemaphoreType.DMA((len(inputs),)),
        ]
        + [pltpu.VMEM((width, n), f32) for n in blocks],
        input_output_aliases={6 + len(inputs): 0} if has_start and not pieces else {},
        compiler_params=pltpu.CompilerParams(vmem_limit_bytes=32 * 2**20),
        cost_estimate=pl.CostEstimate(
            flops=6 * width * W * W * tile_guess, bytes_accessed=4 * W * W * tile_guess, transcendentals=0
        ),
        name="rows_sweep" if by_rows else "cols_sweep",
    )(starts, *tables, integrals, *inputs, *([start] if has_start else []))


def ring_order(n):
    return list(range(0, n, 2)) + list(range(n - 1, 0, -2))


def bit_reverse(value, bits):
    out = jnp.zeros_like(value)
    for b in range(bits):
        out = out + ((value >> b) & 1) * (1 << (bits - 1 - b))
    return out


def tile_tables(tile_mask, order, res_at, con_at, n_con, strip_tiles):
    down, across = tile_mask.shape
    n = len(order)
    ring = jnp.array(order, jnp.int32)
    my_place = jnp.sum(jnp.where(ring == res_at, jnp.arange(n, dtype=jnp.int32), 0))
    steps = [0]
    for s in range(1, n // 2):
        steps += [-s, s]
    steps.append(n // 2)
    places = lax.rem(my_place + jnp.array(steps, jnp.int32) + n, n)
    owners = jnp.sum(jnp.where(places[:, None] == jnp.arange(n, dtype=jnp.int32)[None, :], ring[None, :], 0), axis=1)
    cols = (owners[:, None] * strip_tiles + jnp.arange(strip_tiles, dtype=jnp.int32)[None, :]).reshape(across)
    chosen = (cols[:, None] == jnp.arange(across, dtype=jnp.int32)[None, :]).astype(f32)
    kept = lax.dot_general(chosen, (tile_mask != 0).astype(f32), (((1,), (1,)), ((), ())), preferred_element_type=f32)
    flags = kept.reshape(across * down).astype(jnp.int32)
    total = across * down
    entry = jnp.arange(total, dtype=jnp.int32)
    before = jnp.sum(jnp.where(entry[None, :] < entry[:, None], flags[None, :], 0), axis=1)
    slot = jnp.where(flags > 0, before, total)
    listed = jnp.sum(jnp.where(slot[None, :] == entry[:, None], entry[None, :], 0), axis=1)
    strip = listed // down
    row = listed - strip * down
    col = jnp.sum(jnp.where(strip[:, None] == jnp.arange(across, dtype=jnp.int32)[None, :], cols[None, :], 0), axis=1)
    bits = n_con.bit_length() - 1
    piece = row // strip_tiles
    place = bit_reverse(piece ^ con_at, bits) * strip_tiles + (row - piece * strip_tiles)
    edges = jnp.arange(n + 1, dtype=jnp.int32) * (strip_tiles * down)
    starts = jnp.sum(jnp.where(entry[None, :] < edges[:, None], flags[None, :], 0), axis=1)
    return (row, col, strip, place), starts


def vir_energies(vir_index, eps_vir, offset, count):
    picked = lax.dynamic_slice_in_dim(vir_index, offset, count, 1)
    orbitals = lax.broadcasted_iota(jnp.int32, (eps_vir.shape[0], 1), 0)
    table = eps_vir[:, None]
    first = jnp.sum(jnp.where(picked[0][None, :] == orbitals, table, 0.0), axis=0)
    second = jnp.sum(jnp.where(picked[1][None, :] == orbitals, table, 0.0), axis=0)
    return first + second


def tiled(
    integrals, tile_mask, amplitudes, other_first, other_second, vir_index, occ_index, partner, eps_vir, eps_occ
):
    n_con = lax.axis_size("con")
    n_res = lax.axis_size("res")
    con_at = lax.axis_index("con")
    res_at = lax.axis_index("res")
    fine, occ_cols = amplitudes.shape
    rows, _ = integrals.shape
    strip_tiles = fine // W
    pairs = occ_cols // 2
    width = pairs // PARTS
    parts = range(PARTS)

    column = jnp.arange(occ_cols, dtype=jnp.int32)
    lead = column < partner
    low = jnp.minimum(column, partner)
    pair_of = jnp.sum(jnp.where(column[None, :] < low[:, None], lead[None, :].astype(jnp.int32), 0), axis=1)
    is_pair = jnp.arange(pairs, dtype=jnp.int32)[:, None] == pair_of[None, :]
    chosen = (is_pair & lead[None, :]).astype(f32)
    signed = jnp.where(is_pair, jnp.where(lead, 1.0, -1.0)[None, :], 0.0).astype(f32)

    def compact(value):
        return lax.dot_general(
            signed, value, (((1,), (1,)), ((), ())), precision=precise, preferred_element_type=f32
        )

    def expand(value):
        return lax.dot_general(
            value, signed, (((0,), (0,)), ((), ())), precision=precise, preferred_element_type=f32
        )

    occ_orbitals = lax.broadcasted_iota(jnp.int32, (eps_occ.shape[0], 1), 0)
    occ_energy = jnp.sum(jnp.where(occ_index[0][None, :] == occ_orbitals, eps_occ[:, None], 0.0), axis=0) + jnp.sum(
        jnp.where(occ_index[1][None, :] == occ_orbitals, eps_occ[:, None], 0.0), axis=0
    )
    occ_pair = jnp.sum(chosen * occ_energy[None, :], axis=1)
    order = ring_order(n_res)
    onward = [(order[i], order[(i + 1) % n_res]) for i in range(n_res)]
    backward = [(b, a) for a, b in onward]
    tables, starts = tile_tables(tile_mask, order, res_at, con_at, n_con, strip_tiles)
    rows_sweep = functools.partial(sweep, True, tables, starts)
    cols_sweep = functools.partial(sweep, False, tables, starts)

    def cut(value):
        return [value[p * width : (p + 1) * width] for p in parts]

    def send(values, axis, perm):
        return [lax.ppermute(value, axis, perm) for value in values]

    def scales(index, offset):
        return cut(vir_energies(index, eps_vir, offset, fine)[None, :] - occ_pair[:, None])

    near = n_res // 2
    own = [compact(amplitudes)]
    ahead = behind = own
    blocks = [own]
    ladder = None
    for s in range(1, near):
        ahead, behind = send(ahead, "res", onward), send(behind, "res", backward)
        blocks += [ahead, behind]
        edge = (2 * s + 1 - len(blocks), 2 * s + 1)
        ladder = rows_sweep(edge, strip_tiles, integrals, blocks, rows, ladder)
        blocks = []
    far = send(cut(ahead[0])[: PARTS // 2], "res", onward)
    far += send(cut(behind[0])[PARTS // 2 :], "res", backward)
    pieces = rows_sweep((n_res - 1, n_res), strip_tiles, integrals, [far], rows, ladder, pieces=2)
    kept, sent = pieces[:PARTS], pieces[PARTS:]
    first_other = compact(other_first)
    bit = 1
    while bit < n_con:
        swap = [(i, i ^ bit) for i in range(n_con)]
        came = send(sent, "con", swap)
        bit *= 2
        if bit < n_con:
            mid = kept[0].shape[1] // 2
            sent = [kept[p][:, mid:] + came[p][:, mid:] for p in parts]
            kept = [kept[p][:, :mid] + came[p][:, :mid] for p in parts]
            late_index, late_other, sent[0] = lax.optimization_barrier((vir_index, other_second, sent[0]))
    ready = (
        scales(late_index, (res_at * n_con + con_at) * fine),
        scales(late_index, (con_at * n_res + res_at) * fine),
        cut(compact(late_other)),
    )
    first_scale, second_scale, second_other = lax.optimization_barrier(ready)
    firsts = []
    for p, part in enumerate(cut(first_other)):
        if firsts:
            came[p], firsts[-1] = lax.optimization_barrier((came[p], firsts[-1]))
        firsts.append(0.5 * (part + (kept[p] + came[p])) / first_scale[p])
    held = [firsts]
    while bit > 1:
        bit //= 2
        swap = [(i, i ^ bit) for i in range(n_con)]
        block = [jnp.concatenate([h[p] for h in held], axis=1) if len(held) > 1 else held[0][p] for p in parts]
        held = held + [send(block[:-1], "con", swap) + send(block[-1:], "con", swap)]
    first_out = expand(jnp.concatenate(firsts, axis=0))
    far = cols_sweep((n_res - 1, n_res), strip_tiles, integrals, held, fine, pieces=1)
    ahead = [lax.ppermute(far[p], "res", onward) if p < PARTS // 2 else None for p in parts]
    behind = [None if p < PARTS // 2 else lax.ppermute(far[p], "res", backward) for p in parts]
    for s in range(near - 1, 0, -1):
        edge = (2 * s - 1, 2 * s + 1)
        both = cols_sweep(edge, strip_tiles, integrals, held, 2 * fine, pieces=2)
        to_behind, to_ahead = both[:PARTS], both[PARTS:]
        ahead = send([to_ahead[p] if ahead[p] is None else to_ahead[p] + ahead[p] for p in parts], "res", onward)
        behind = send([to_behind[p] if behind[p] is None else to_behind[p] + behind[p] for p in parts], "res", backward)
    mine = cols_sweep((0, 1), strip_tiles, integrals, held, fine, pieces=1)
    seconds = [
        (0.5 * second_other[p] + ((mine[p] + ahead[p]) + behind[p])) / second_scale[p] for p in parts
    ]
    return first_out, expand(jnp.concatenate(seconds, axis=0))


def per_device(integrals, tile_mask, amplitudes, *rest):
    n_con = lax.axis_size("con")
    n_res = lax.axis_size("res")
    fits = (
        amplitudes.shape[0] % W == 0
        and amplitudes.shape[1] % (32 * PARTS) == 0
        and n_con & (n_con - 1) == 0
        and n_res % 2 == 0
        and n_res > 2
    )
    if not fits:
        return general(integrals, tile_mask, amplitudes, *rest)
    return tiled(integrals, tile_mask, amplitudes, *rest)


def solution(mesh):
    return jax.shard_map(
        per_device,
        mesh=mesh,
        in_specs=(
            P("res", "con"),
            P("res", "con"),
            P(("con", "res"), None),
            P(("res", "con"), None),
            P(("con", "res"), None),
            P(),
            P(),
            P(),
            P(),
            P(),
        ),
        out_specs=(P(("res", "con"), None), P(("con", "res"), None)),
        check_vma=False,
    )
```

```python
import functools

import jax
import jax.numpy as jnp
from jax import lax
from jax.experimental import pallas as pl
from jax.experimental.pallas import tpu as pltpu
from jax.sharding import PartitionSpec as P


W = 256
PARTS = 2
DEPTH = 12
UNROLL = 4


f32 = jnp.float32
bf16 = jnp.bfloat16
precise = lax.Precision.HIGHEST


def pair_energy(pair_index, table):
    orbitals = lax.broadcasted_iota(jnp.int32, (1, table.shape[0]), 1)
    counts = (pair_index[0][:, None] == orbitals).astype(f32) + (pair_index[1][:, None] == orbitals).astype(f32)
    return jnp.dot(counts, table, precision=precise, preferred_element_type=f32)


def renew(ladder, other, vir_rows, occ_energy, swap_matrix):
    unscaled = (other + ladder) / (vir_rows[:, None] - occ_energy[None, :])
    swapped = jnp.dot(unscaled, swap_matrix, precision=precise, preferred_element_type=f32)
    return 0.5 * (unscaled - swapped)


def general(
    integrals, tile_mask, amplitudes, other_first, other_second, vir_index, occ_index, partner, eps_vir, eps_occ
):
    row_count, col_count = integrals.shape
    tiles_down, tiles_across = tile_mask.shape
    weights = tile_mask.astype(f32)
    screened = (integrals.reshape(tiles_down, W, tiles_across, W) * weights[:, None, :, None]).reshape(
        row_count, col_count
    )
    occ_energy = pair_energy(occ_index, eps_occ)
    occ_cols = amplitudes.shape[1]
    column_ids = lax.broadcasted_iota(jnp.int32, (occ_cols, occ_cols), 0)
    swap_matrix = (column_ids == partner[None, :]).astype(f32)
    n_con = lax.axis_size("con")
    n_res = lax.axis_size("res")
    con_at = lax.axis_index("con")
    res_at = lax.axis_index("res")
    fine_rows = amplitudes.shape[0]

    def vir_rows(offset):
        return pair_energy(lax.dynamic_slice_in_dim(vir_index, offset, fine_rows, 1), eps_vir)

    partial_one = jnp.dot(
        screened,
        lax.all_gather(amplitudes, "res", axis=0, tiled=True),
        precision=precise,
        preferred_element_type=f32,
    )
    ladder_one = lax.psum_scatter(partial_one, "con", scatter_dimension=0, tiled=True)
    first_vir = vir_rows((res_at * n_con + con_at) * fine_rows)
    first_update = renew(ladder_one, other_first, first_vir, occ_energy, swap_matrix)
    partial_two = lax.dot_general(
        screened,
        lax.all_gather(first_update, "con", axis=0, tiled=True),
        (((0,), (0,)), ((), ())),
        precision=precise,
        preferred_element_type=f32,
    )
    ladder_two = lax.psum_scatter(partial_two, "res", scatter_dimension=0, tiled=True)
    second_vir = vir_rows((con_at * n_res + res_at) * fine_rows)
    second_update = renew(ladder_two, other_second, second_vir, occ_energy, swap_matrix)
    return (first_update, second_update)


def halves(value):
    high = value.astype(bf16)
    return high, (value - high.astype(f32)).astype(bf16)


def sweep_kernel(
    by_rows, blocks, n_parts, has_start, n_out, keeps, strip_base, edge,
    starts, row_of, col_of, strip_of, place_of, a_hbm, *refs,
):
    n_x = len(blocks) * n_parts
    x_refs = refs[:n_x]
    start_ref = refs[n_x] if has_start else None
    refs = refs[n_x + has_start :]
    if not blocks:
        x_split, refs = refs[0], refs[1:]
    out_refs, refs = refs[:n_out], refs[n_out:]
    if keeps:
        x_split, refs = refs[0], refs[1:]
    y_ref = out_refs[0] if n_out == 1 else refs[0]
    refs = refs if n_out == 1 else refs[1:]
    tiles, sems, x_sem = refs[:3]
    x_whole = refs[3:]
    if blocks and not keeps:
        x_split, x_whole = x_whole[0], x_whole[1:]
    first = starts[edge[0]]
    count = starts[edge[1]] - first

    def fetch(i):
        entry = first + i
        rows = pl.ds(pl.multiple_of(row_of[entry] * W, W), W)
        cols = pl.ds(pl.multiple_of(col_of[entry] * W, W), W)
        slot = lax.rem(i, DEPTH)
        return pltpu.make_async_copy(a_hbm.at[rows, cols], tiles.at[slot], sems.at[slot])

    part_rows = y_ref.shape[0] // n_parts
    loads = []
    for n in range(n_x):
        part = pl.ds((n % n_parts) * part_rows, part_rows)
        loads.append(pltpu.make_async_copy(x_refs[n], x_whole[n // n_parts].at[part, :], x_sem.at[n]))
        loads[-1].start()
    for i in range(DEPTH):

        @pl.when(i < count)
        def _():
            fetch(i).start()

    y_ref[...] = start_ref[...] if has_start else jnp.zeros_like(y_ref)
    width = y_ref.shape[0]
    at = 0
    for n in range(len(blocks)):
        for p in range(n_parts):
            loads[n * n_parts + p].wait()
        for j in range(blocks[n] // W):
            high, low = halves(x_whole[n][:, j * W : (j + 1) * W])
            x_split[at, :width, :] = high
            x_split[at, width:, :] = low
            at += 1

    def product(i):
        entry = first + i
        high, low = halves(tiles[lax.rem(i, DEPTH)])
        strip = strip_of[entry] - strip_base
        place = place_of[entry]
        source, target = (strip, place) if by_rows else (place, strip)
        dims = (((1,), (1 if by_rows else 0,)), ((), ()))
        both = x_split[source]
        main = lax.dot_general(both, high, dims, preferred_element_type=f32)
        rest = lax.dot_general(both[:width], low, dims, preferred_element_type=f32)
        return (main[:width] + main[width:]) + rest, pl.ds(pl.multiple_of(target * W, W), W)

    def several(block, _):
        at = block * UNROLL
        for u in range(UNROLL):
            fetch(at + u).wait()
        done = [product(at + u) for u in range(UNROLL)]
        for value, where in done:
            y_ref[:, where] += value
        for u in range(UNROLL):

            @pl.when(at + u + DEPTH < count)
            def _():
                fetch(at + u + DEPTH).start()

        return 0

    def single(i, _):
        fetch(i).wait()
        value, where = product(i)
        y_ref[:, where] += value
        return 0

    several_of = count // UNROLL
    lax.fori_loop(0, several_of, several, 0)
    lax.fori_loop(several_of * UNROLL, count, single, 0)
    if n_out > 1:
        out_cols = out_refs[0].shape[1]
        for n, out_ref in enumerate(out_refs):
            p, c = n % n_parts, n // n_parts
            out_ref[...] = y_ref[p * part_rows : (p + 1) * part_rows, c * out_cols : (c + 1) * out_cols]


def sweep(
    by_rows, tables, starts, edge, strip_tiles, integrals, x_blocks, y_width, start=None, pieces=0, split=None, keeps=False
):
    n_parts = len(x_blocks[0]) if split is None else PARTS
    width = sum(part.shape[0] for part in x_blocks[0]) if split is None else split.shape[1] // 2
    blocks = [block[0].shape[1] for block in x_blocks] if split is None else []
    inputs = [part for block in x_blocks for part in block] if split is None else []
    scalar = pl.BlockSpec(memory_space=pltpu.SMEM)
    vector = pl.BlockSpec(memory_space=pltpu.VMEM)
    anywhere = pl.BlockSpec(memory_space=pl.ANY)
    has_start = start is not None
    n_out = pieces * n_parts if pieces else 1
    tile_guess = (edge[1] - edge[0]) * strip_tiles * (integrals.shape[0] // W) // 2
    split_shape = (sum(blocks) // W, 2 * width, W)
    out_shape = [jax.ShapeDtypeStruct((width, y_width), f32)]
    if pieces:
        out_shape = [jax.ShapeDtypeStruct((width // n_parts, y_width // pieces), f32)] * n_out
    if keeps:
        out_shape += [jax.ShapeDtypeStruct(split_shape, bf16)]
    late = ([start] if has_start else []) + ([] if split is None else [split])
    out = pl.pallas_call(
        functools.partial(
            sweep_kernel, by_rows, blocks, n_parts, int(has_start), n_out, keeps, edge[0] * strip_tiles, edge
        ),
        out_shape=out_shape,
        in_specs=[scalar] * 5 + [anywhere] * (1 + len(inputs)) + [vector] * len(late),
        out_specs=[vector] * len(out_shape),
        scratch_shapes=([pltpu.VMEM((width, y_width), f32)] if n_out > 1 else [])
        + [
            pltpu.VMEM((DEPTH, W, W), f32),
            pltpu.SemaphoreType.DMA((DEPTH,)),
            pltpu.SemaphoreType.DMA((max(len(inputs), 1),)),
        ]
        + ([pltpu.VMEM(split_shape, bf16)] if blocks and not keeps else [])
        + [pltpu.VMEM((width, n), f32) for n in blocks],
        input_output_aliases={6 + len(inputs): 0} if has_start and not pieces else {},
        compiler_params=pltpu.CompilerParams(vmem_limit_bytes=32 * 2**20),
        cost_estimate=pl.CostEstimate(
            flops=6 * width * W * W * tile_guess, bytes_accessed=4 * W * W * tile_guess, transcendentals=0
        ),
        name="rows_sweep" if by_rows else "cols_sweep",
    )(starts, *tables, integrals, *inputs, *late)
    return out if len(out) > 1 else out[0]


def ring_order(n):
    return list(range(0, n, 2)) + list(range(n - 1, 0, -2))


def bit_reverse(value, bits):
    out = jnp.zeros_like(value)
    for b in range(bits):
        out = out + ((value >> b) & 1) * (1 << (bits - 1 - b))
    return out


def tile_tables(tile_mask, order, res_at, con_at, n_con, strip_tiles):
    down, across = tile_mask.shape
    n = len(order)
    ring = jnp.array(order, jnp.int32)
    my_place = jnp.sum(jnp.where(ring == res_at, jnp.arange(n, dtype=jnp.int32), 0))
    steps = [0]
    for s in range(1, n // 2):
        steps += [-s, s]
    steps.append(n // 2)
    places = lax.rem(my_place + jnp.array(steps, jnp.int32) + n, n)
    owners = jnp.sum(jnp.where(places[:, None] == jnp.arange(n, dtype=jnp.int32)[None, :], ring[None, :], 0), axis=1)
    cols = (owners[:, None] * strip_tiles + jnp.arange(strip_tiles, dtype=jnp.int32)[None, :]).reshape(across)
    chosen = (cols[:, None] == jnp.arange(across, dtype=jnp.int32)[None, :]).astype(f32)
    kept = lax.dot_general(chosen, (tile_mask != 0).astype(f32), (((1,), (1,)), ((), ())), preferred_element_type=f32)
    flags = kept.reshape(across * down).astype(jnp.int32)
    total = across * down
    entry = jnp.arange(total, dtype=jnp.int32)
    before = jnp.sum(jnp.where(entry[None, :] < entry[:, None], flags[None, :], 0), axis=1)
    slot = jnp.where(flags > 0, before, total)
    listed = jnp.sum(jnp.where(slot[None, :] == entry[:, None], entry[None, :], 0), axis=1)
    strip = listed // down
    row = listed - strip * down
    col = jnp.sum(jnp.where(strip[:, None] == jnp.arange(across, dtype=jnp.int32)[None, :], cols[None, :], 0), axis=1)
    bits = n_con.bit_length() - 1
    piece = row // strip_tiles
    place = bit_reverse(piece ^ con_at, bits) * strip_tiles + (row - piece * strip_tiles)
    edges = jnp.arange(n + 1, dtype=jnp.int32) * (strip_tiles * down)
    starts = jnp.sum(jnp.where(entry[None, :] < edges[:, None], flags[None, :], 0), axis=1)
    return (row, col, strip, place), starts


def vir_energies(vir_index, eps_vir, offset, count):
    picked = lax.dynamic_slice_in_dim(vir_index, offset, count, 1)
    orbitals = lax.broadcasted_iota(jnp.int32, (eps_vir.shape[0], 1), 0)
    table = eps_vir[:, None]
    first = jnp.sum(jnp.where(picked[0][None, :] == orbitals, table, 0.0), axis=0)
    second = jnp.sum(jnp.where(picked[1][None, :] == orbitals, table, 0.0), axis=0)
    return first + second


def tiled(
    integrals, tile_mask, amplitudes, other_first, other_second, vir_index, occ_index, partner, eps_vir, eps_occ
):
    n_con = lax.axis_size("con")
    n_res = lax.axis_size("res")
    con_at = lax.axis_index("con")
    res_at = lax.axis_index("res")
    fine, occ_cols = amplitudes.shape
    rows, _ = integrals.shape
    strip_tiles = fine // W
    pairs = occ_cols // 2
    width = pairs // PARTS
    parts = range(PARTS)

    column = jnp.arange(occ_cols, dtype=jnp.int32)
    lead = column < partner
    low = jnp.minimum(column, partner)
    pair_of = jnp.sum(jnp.where(column[None, :] < low[:, None], lead[None, :].astype(jnp.int32), 0), axis=1)
    is_pair = jnp.arange(pairs, dtype=jnp.int32)[:, None] == pair_of[None, :]
    chosen = (is_pair & lead[None, :]).astype(f32)
    signed = jnp.where(is_pair, jnp.where(lead, 1.0, -1.0)[None, :], 0.0).astype(f32)

    def compact(value):
        return lax.dot_general(
            signed, value, (((1,), (1,)), ((), ())), precision=precise, preferred_element_type=f32
        )

    def expand(value):
        return lax.dot_general(
            value, signed, (((0,), (0,)), ((), ())), precision=precise, preferred_element_type=f32
        )

    occ_orbitals = lax.broadcasted_iota(jnp.int32, (eps_occ.shape[0], 1), 0)
    occ_energy = jnp.sum(jnp.where(occ_index[0][None, :] == occ_orbitals, eps_occ[:, None], 0.0), axis=0) + jnp.sum(
        jnp.where(occ_index[1][None, :] == occ_orbitals, eps_occ[:, None], 0.0), axis=0
    )
    occ_pair = jnp.sum(chosen * occ_energy[None, :], axis=1)
    order = ring_order(n_res)
    onward = [(order[i], order[(i + 1) % n_res]) for i in range(n_res)]
    backward = [(b, a) for a, b in onward]
    tables, starts = tile_tables(tile_mask, order, res_at, con_at, n_con, strip_tiles)
    rows_sweep = functools.partial(sweep, True, tables, starts)
    cols_sweep = functools.partial(sweep, False, tables, starts)

    def cut(value):
        return [value[p * width : (p + 1) * width] for p in parts]

    def send(values, axis, perm):
        return [lax.ppermute(value, axis, perm) for value in values]

    def scales(index, offset):
        return cut(vir_energies(index, eps_vir, offset, fine)[None, :] - occ_pair[:, None])

    near = n_res // 2
    own = cut(compact(amplitudes))
    first_other, second_other = compact(other_first), compact(other_second)
    ahead = behind = own
    ladder = rows_sweep((0, 1), strip_tiles, integrals, [own], rows)
    for s in range(1, near):
        ahead, behind = send(ahead, "res", onward), send(behind, "res", backward)
        ahead, behind = lax.optimization_barrier((ahead, behind))
        ladder = rows_sweep((2 * s - 1, 2 * s + 1), strip_tiles, integrals, [ahead, behind], rows, ladder)
    far = send(ahead[: PARTS // 2], "res", onward)
    far += send(behind[PARTS // 2 :], "res", backward)
    pieces = rows_sweep((n_res - 1, n_res), strip_tiles, integrals, [far], rows, ladder, pieces=2)
    kept, sent = pieces[:PARTS], pieces[PARTS:]
    bit = 1
    while bit < n_con:
        swap = [(i, i ^ bit) for i in range(n_con)]
        came = send(sent, "con", swap)
        bit *= 2
        if bit < n_con:
            mid = kept[0].shape[1] // 2
            sent = [kept[p][:, mid:] + came[p][:, mid:] for p in parts]
            kept = [kept[p][:, :mid] + came[p][:, :mid] for p in parts]
            late_index, sent[0] = lax.optimization_barrier((vir_index, sent[0]))
    ready = (
        scales(late_index, (res_at * n_con + con_at) * fine),
        scales(late_index, (con_at * n_res + res_at) * fine),
    )
    first_scale, second_scale = lax.optimization_barrier(ready)
    firsts = []
    for p, part in enumerate(cut(first_other)):
        if firsts:
            came[p], firsts[-1] = lax.optimization_barrier((came[p], firsts[-1]))
        firsts.append(0.5 * (part + (kept[p] + came[p])) / first_scale[p])
    held = [firsts]
    while bit > 1:
        bit //= 2
        swap = [(i, i ^ bit) for i in range(n_con)]
        block = [jnp.concatenate([h[p] for h in held], axis=1) if len(held) > 1 else held[0][p] for p in parts]
        held = held + [send(block[:-1], "con", swap) + send(block[-1:], "con", swap)]
    first_out = expand(jnp.concatenate(firsts, axis=0))
    *far, split = cols_sweep((n_res - 1, n_res), strip_tiles, integrals, held, fine, pieces=1, keeps=True)
    ahead = [lax.ppermute(far[p], "res", onward) if p < PARTS // 2 else None for p in parts]
    behind = [None if p < PARTS // 2 else lax.ppermute(far[p], "res", backward) for p in parts]
    for s in range(near - 1, 0, -1):
        edge = (2 * s - 1, 2 * s + 1)
        both = cols_sweep(edge, strip_tiles, integrals, None, 2 * fine, pieces=2, split=split)
        to_behind, to_ahead = both[:PARTS], both[PARTS:]
        ahead = send([to_ahead[p] if ahead[p] is None else to_ahead[p] + ahead[p] for p in parts], "res", onward)
        behind = send([to_behind[p] if behind[p] is None else to_behind[p] + behind[p] for p in parts], "res", backward)
    mine = cols_sweep((0, 1), strip_tiles, integrals, None, fine, pieces=1, split=split)
    second_other = cut(second_other)
    seconds = [
        (0.5 * second_other[p] + ((mine[p] + ahead[p]) + behind[p])) / second_scale[p] for p in parts
    ]
    return first_out, expand(jnp.concatenate(seconds, axis=0))


def per_device(integrals, tile_mask, amplitudes, *rest):
    n_con = lax.axis_size("con")
    n_res = lax.axis_size("res")
    fits = (
        amplitudes.shape[0] % W == 0
        and amplitudes.shape[1] % (32 * PARTS) == 0
        and n_con & (n_con - 1) == 0
        and n_res % 2 == 0
        and n_res > 2
    )
    if not fits:
        return general(integrals, tile_mask, amplitudes, *rest)
    return tiled(integrals, tile_mask, amplitudes, *rest)


def solution(mesh):
    return jax.shard_map(
        per_device,
        mesh=mesh,
        in_specs=(
            P("res", "con"),
            P("res", "con"),
            P(("con", "res"), None),
            P(("res", "con"), None),
            P(("con", "res"), None),
            P(),
            P(),
            P(),
            P(),
            P(),
        ),
        out_specs=(P(("res", "con"), None), P(("con", "res"), None)),
        check_vma=False,
    )
```

```python
import functools

import jax
import jax.numpy as jnp
from jax import lax
from jax.experimental import pallas as pl
from jax.experimental.pallas import tpu as pltpu
from jax.sharding import PartitionSpec as P


W = 256
PARTS = 2
DEPTH = 12
UNROLL = 4


f32 = jnp.float32
bf16 = jnp.bfloat16
precise = lax.Precision.HIGHEST


def pair_energy(pair_index, table):
    orbitals = lax.broadcasted_iota(jnp.int32, (1, table.shape[0]), 1)
    counts = (pair_index[0][:, None] == orbitals).astype(f32) + (pair_index[1][:, None] == orbitals).astype(f32)
    return jnp.dot(counts, table, precision=precise, preferred_element_type=f32)


def renew(ladder, other, vir_rows, occ_energy, swap_matrix):
    unscaled = (other + ladder) / (vir_rows[:, None] - occ_energy[None, :])
    swapped = jnp.dot(unscaled, swap_matrix, precision=precise, preferred_element_type=f32)
    return 0.5 * (unscaled - swapped)


def general(
    integrals, tile_mask, amplitudes, other_first, other_second, vir_index, occ_index, partner, eps_vir, eps_occ
):
    row_count, col_count = integrals.shape
    tiles_down, tiles_across = tile_mask.shape
    weights = tile_mask.astype(f32)
    screened = (integrals.reshape(tiles_down, W, tiles_across, W) * weights[:, None, :, None]).reshape(
        row_count, col_count
    )
    occ_energy = pair_energy(occ_index, eps_occ)
    occ_cols = amplitudes.shape[1]
    column_ids = lax.broadcasted_iota(jnp.int32, (occ_cols, occ_cols), 0)
    swap_matrix = (column_ids == partner[None, :]).astype(f32)
    n_con = lax.axis_size("con")
    n_res = lax.axis_size("res")
    con_at = lax.axis_index("con")
    res_at = lax.axis_index("res")
    fine_rows = amplitudes.shape[0]

    def vir_rows(offset):
        return pair_energy(lax.dynamic_slice_in_dim(vir_index, offset, fine_rows, 1), eps_vir)

    partial_one = jnp.dot(
        screened,
        lax.all_gather(amplitudes, "res", axis=0, tiled=True),
        precision=precise,
        preferred_element_type=f32,
    )
    ladder_one = lax.psum_scatter(partial_one, "con", scatter_dimension=0, tiled=True)
    first_vir = vir_rows((res_at * n_con + con_at) * fine_rows)
    first_update = renew(ladder_one, other_first, first_vir, occ_energy, swap_matrix)
    partial_two = lax.dot_general(
        screened,
        lax.all_gather(first_update, "con", axis=0, tiled=True),
        (((0,), (0,)), ((), ())),
        precision=precise,
        preferred_element_type=f32,
    )
    ladder_two = lax.psum_scatter(partial_two, "res", scatter_dimension=0, tiled=True)
    second_vir = vir_rows((con_at * n_res + res_at) * fine_rows)
    second_update = renew(ladder_two, other_second, second_vir, occ_energy, swap_matrix)
    return (first_update, second_update)


def halves(value):
    high = value.astype(bf16)
    return high, (value - high.astype(f32)).astype(bf16)


def sweep_kernel(
    by_rows, blocks, n_parts, has_start, n_out, keeps, strip_base, edge,
    starts, row_of, col_of, strip_of, place_of, a_hbm, *refs,
):
    n_x = len(blocks) * n_parts
    x_refs = refs[:n_x]
    start_ref = refs[n_x] if has_start else None
    refs = refs[n_x + has_start :]
    if not blocks:
        x_split, refs = refs[0], refs[1:]
    out_refs, refs = refs[:n_out], refs[n_out:]
    if keeps:
        x_split, refs = refs[0], refs[1:]
    y_ref = out_refs[0] if n_out == 1 else refs[0]
    refs = refs if n_out == 1 else refs[1:]
    tiles, sems, x_sem = refs[:3]
    x_whole = refs[3:]
    if blocks and not keeps:
        x_split, x_whole = x_whole[0], x_whole[1:]
    first = starts[edge[0]]
    count = starts[edge[1]] - first

    def fetch(i):
        entry = first + i
        rows = pl.ds(pl.multiple_of(row_of[entry] * W, W), W)
        cols = pl.ds(pl.multiple_of(col_of[entry] * W, W), W)
        slot = lax.rem(i, DEPTH)
        return pltpu.make_async_copy(a_hbm.at[rows, cols], tiles.at[slot], sems.at[slot])

    part_rows = y_ref.shape[0] // n_parts
    loads = []
    for n in range(n_x):
        part = pl.ds((n % n_parts) * part_rows, part_rows)
        loads.append(pltpu.make_async_copy(x_refs[n], x_whole[n // n_parts].at[part, :], x_sem.at[n]))
        loads[-1].start()
    for i in range(DEPTH):

        @pl.when(i < count)
        def _():
            fetch(i).start()

    y_ref[...] = start_ref[...] if has_start else jnp.zeros_like(y_ref)
    width = y_ref.shape[0]
    at = 0
    for n in range(len(blocks)):
        for p in range(n_parts):
            loads[n * n_parts + p].wait()
        for j in range(blocks[n] // W):
            high, low = halves(x_whole[n][:, j * W : (j + 1) * W])
            x_split[at, :width, :] = high
            x_split[at, width:, :] = low
            at += 1

    def product(i):
        entry = first + i
        high, low = halves(tiles[lax.rem(i, DEPTH)])
        strip = strip_of[entry] - strip_base
        place = place_of[entry]
        source, target = (strip, place) if by_rows else (place, strip)
        dims = (((1,), (1 if by_rows else 0,)), ((), ()))
        both = x_split[source]
        main = lax.dot_general(both, high, dims, preferred_element_type=f32)
        rest = lax.dot_general(both[:width], low, dims, preferred_element_type=f32)
        return (main[:width] + main[width:]) + rest, pl.ds(pl.multiple_of(target * W, W), W)

    def several(block, _):
        at = block * UNROLL
        for u in range(UNROLL):
            fetch(at + u).wait()
        done = [product(at + u) for u in range(UNROLL)]
        for value, where in done:
            y_ref[:, where] += value
        for u in range(UNROLL):

            @pl.when(at + u + DEPTH < count)
            def _():
                fetch(at + u + DEPTH).start()

        return 0

    def single(i, _):
        fetch(i).wait()
        value, where = product(i)
        y_ref[:, where] += value
        return 0

    several_of = count // UNROLL
    lax.fori_loop(0, several_of, several, 0)
    lax.fori_loop(several_of * UNROLL, count, single, 0)
    if n_out > 1:
        out_cols = out_refs[0].shape[1]
        for n, out_ref in enumerate(out_refs):
            p, c = n % n_parts, n // n_parts
            out_ref[...] = y_ref[p * part_rows : (p + 1) * part_rows, c * out_cols : (c + 1) * out_cols]


def sweep(
    by_rows, tables, starts, edge, strip_tiles, integrals, x_blocks, y_width, start=None, pieces=0, split=None, keeps=False
):
    n_parts = len(x_blocks[0]) if split is None else PARTS
    width = sum(part.shape[0] for part in x_blocks[0]) if split is None else split.shape[1] // 2
    blocks = [block[0].shape[1] for block in x_blocks] if split is None else []
    inputs = [part for block in x_blocks for part in block] if split is None else []
    scalar = pl.BlockSpec(memory_space=pltpu.SMEM)
    vector = pl.BlockSpec(memory_space=pltpu.VMEM)
    anywhere = pl.BlockSpec(memory_space=pl.ANY)
    has_start = start is not None
    n_out = pieces * n_parts if pieces else 1
    tile_guess = (edge[1] - edge[0]) * strip_tiles * (integrals.shape[0] // W) // 2
    split_shape = (sum(blocks) // W, 2 * width, W)
    out_shape = [jax.ShapeDtypeStruct((width, y_width), f32)]
    if pieces:
        out_shape = [jax.ShapeDtypeStruct((width // n_parts, y_width // pieces), f32)] * n_out
    if keeps:
        out_shape += [jax.ShapeDtypeStruct(split_shape, bf16)]
    late = ([start] if has_start else []) + ([] if split is None else [split])
    out = pl.pallas_call(
        functools.partial(
            sweep_kernel, by_rows, blocks, n_parts, int(has_start), n_out, keeps, edge[0] * strip_tiles, edge
        ),
        out_shape=out_shape,
        in_specs=[scalar] * 5 + [anywhere] * (1 + len(inputs)) + [vector] * len(late),
        out_specs=[vector] * len(out_shape),
        scratch_shapes=([pltpu.VMEM((width, y_width), f32)] if n_out > 1 else [])
        + [
            pltpu.VMEM((DEPTH, W, W), f32),
            pltpu.SemaphoreType.DMA((DEPTH,)),
            pltpu.SemaphoreType.DMA((max(len(inputs), 1),)),
        ]
        + ([pltpu.VMEM(split_shape, bf16)] if blocks and not keeps else [])
        + [pltpu.VMEM((width, n), f32) for n in blocks],
        input_output_aliases={6 + len(inputs): 0} if has_start and not pieces else {},
        compiler_params=pltpu.CompilerParams(vmem_limit_bytes=32 * 2**20),
        cost_estimate=pl.CostEstimate(
            flops=6 * width * W * W * tile_guess, bytes_accessed=4 * W * W * tile_guess, transcendentals=0
        ),
        name="rows_sweep" if by_rows else "cols_sweep",
    )(starts, *tables, integrals, *inputs, *late)
    return out if len(out) > 1 else out[0]


def ring_order(n):
    return list(range(0, n, 2)) + list(range(n - 1, 0, -2))


def bit_reverse(value, bits):
    out = jnp.zeros_like(value)
    for b in range(bits):
        out = out + ((value >> b) & 1) * (1 << (bits - 1 - b))
    return out


def tile_tables(tile_mask, order, res_at, con_at, n_con, strip_tiles):
    down, across = tile_mask.shape
    n = len(order)
    ring = jnp.array(order, jnp.int32)
    my_place = jnp.sum(jnp.where(ring == res_at, jnp.arange(n, dtype=jnp.int32), 0))
    steps = [0]
    for s in range(1, n // 2):
        steps += [-s, s]
    steps.append(n // 2)
    places = lax.rem(my_place + jnp.array(steps, jnp.int32) + n, n)
    owners = jnp.sum(jnp.where(places[:, None] == jnp.arange(n, dtype=jnp.int32)[None, :], ring[None, :], 0), axis=1)
    cols = (owners[:, None] * strip_tiles + jnp.arange(strip_tiles, dtype=jnp.int32)[None, :]).reshape(across)
    chosen = (cols[:, None] == jnp.arange(across, dtype=jnp.int32)[None, :]).astype(f32)
    kept = lax.dot_general(chosen, (tile_mask != 0).astype(f32), (((1,), (1,)), ((), ())), preferred_element_type=f32)
    flags = kept.reshape(across * down).astype(jnp.int32)
    total = across * down
    entry = jnp.arange(total, dtype=jnp.int32)
    before = jnp.sum(jnp.where(entry[None, :] < entry[:, None], flags[None, :], 0), axis=1)
    slot = jnp.where(flags > 0, before, total)
    listed = jnp.sum(jnp.where(slot[None, :] == entry[:, None], entry[None, :], 0), axis=1)
    strip = listed // down
    row = listed - strip * down
    col = jnp.sum(jnp.where(strip[:, None] == jnp.arange(across, dtype=jnp.int32)[None, :], cols[None, :], 0), axis=1)
    bits = n_con.bit_length() - 1
    piece = row // strip_tiles
    place = bit_reverse(piece ^ con_at, bits) * strip_tiles + (row - piece * strip_tiles)
    edges = jnp.arange(n + 1, dtype=jnp.int32) * (strip_tiles * down)
    starts = jnp.sum(jnp.where(entry[None, :] < edges[:, None], flags[None, :], 0), axis=1)
    return (row, col, strip, place), starts


def vir_energies(vir_index, eps_vir, offset, count):
    picked = lax.dynamic_slice_in_dim(vir_index, offset, count, 1)
    orbitals = lax.broadcasted_iota(jnp.int32, (eps_vir.shape[0], 1), 0)
    table = eps_vir[:, None]
    first = jnp.sum(jnp.where(picked[0][None, :] == orbitals, table, 0.0), axis=0)
    second = jnp.sum(jnp.where(picked[1][None, :] == orbitals, table, 0.0), axis=0)
    return first + second


def tiled(
    integrals, tile_mask, amplitudes, other_first, other_second, vir_index, occ_index, partner, eps_vir, eps_occ
):
    n_con = lax.axis_size("con")
    n_res = lax.axis_size("res")
    con_at = lax.axis_index("con")
    res_at = lax.axis_index("res")
    fine, occ_cols = amplitudes.shape
    rows, _ = integrals.shape
    strip_tiles = fine // W
    pairs = occ_cols // 2
    width = pairs // PARTS
    parts = range(PARTS)

    column = jnp.arange(occ_cols, dtype=jnp.int32)
    lead = column < partner
    low = jnp.minimum(column, partner)
    pair_of = jnp.sum(jnp.where(column[None, :] < low[:, None], lead[None, :].astype(jnp.int32), 0), axis=1)
    is_pair = jnp.arange(pairs, dtype=jnp.int32)[:, None] == pair_of[None, :]
    chosen = (is_pair & lead[None, :]).astype(f32)
    signed = jnp.where(is_pair, jnp.where(lead, 1.0, -1.0)[None, :], 0.0).astype(f32)

    def compact(value):
        return lax.dot_general(
            signed, value, (((1,), (1,)), ((), ())), precision=precise, preferred_element_type=f32
        )

    def expand(value):
        return lax.dot_general(
            value, signed, (((0,), (0,)), ((), ())), precision=precise, preferred_element_type=f32
        )

    occ_orbitals = lax.broadcasted_iota(jnp.int32, (eps_occ.shape[0], 1), 0)
    occ_energy = jnp.sum(jnp.where(occ_index[0][None, :] == occ_orbitals, eps_occ[:, None], 0.0), axis=0) + jnp.sum(
        jnp.where(occ_index[1][None, :] == occ_orbitals, eps_occ[:, None], 0.0), axis=0
    )
    occ_pair = jnp.sum(chosen * occ_energy[None, :], axis=1)
    order = ring_order(n_res)
    onward = [(order[i], order[(i + 1) % n_res]) for i in range(n_res)]
    backward = [(b, a) for a, b in onward]
    tables, starts = tile_tables(tile_mask, order, res_at, con_at, n_con, strip_tiles)
    rows_sweep = functools.partial(sweep, True, tables, starts)
    cols_sweep = functools.partial(sweep, False, tables, starts)

    def cut(value):
        return [value[p * width : (p + 1) * width] for p in parts]

    def send(values, axis, perm):
        return [lax.ppermute(value, axis, perm) for value in values]

    def scales(index, offset):
        return cut(vir_energies(index, eps_vir, offset, fine)[None, :] - occ_pair[:, None])

    near = n_res // 2
    own = [compact(amplitudes)]
    first_other = compact(other_first)
    ahead = behind = own
    ladder = rows_sweep((0, 1), strip_tiles, integrals, [own], rows)
    for s in range(1, near):
        if s == near - 1:
            ahead, behind = cut(ahead[0]), cut(behind[0])
        ahead, behind = send(ahead, "res", onward), send(behind, "res", backward)
        ahead, behind = lax.optimization_barrier((ahead, behind))
        ladder = rows_sweep((2 * s - 1, 2 * s + 1), strip_tiles, integrals, [ahead, behind], rows, ladder)
    far = send(ahead[: PARTS // 2], "res", onward)
    far += send(behind[PARTS // 2 :], "res", backward)
    pieces = rows_sweep((n_res - 1, n_res), strip_tiles, integrals, [far], rows, ladder, pieces=2)
    kept, sent = pieces[:PARTS], pieces[PARTS:]
    bit = 1
    while bit < n_con:
        swap = [(i, i ^ bit) for i in range(n_con)]
        came = send(sent[:-1], "con", swap) + send(sent[-1:], "con", swap)
        bit *= 2
        if bit < n_con:
            mid = kept[0].shape[1] // 2
            sent = [kept[p][:, mid:] + came[p][:, mid:] for p in parts]
            kept = [kept[p][:, :mid] + came[p][:, :mid] for p in parts]
            late_index, sent[0] = lax.optimization_barrier((vir_index, sent[0]))
    ready = (
        scales(late_index, (res_at * n_con + con_at) * fine),
        scales(late_index, (con_at * n_res + res_at) * fine),
    )
    first_scale, second_scale = lax.optimization_barrier(ready)
    firsts = []
    for p, part in enumerate(cut(first_other)):
        if firsts:
            came[p], firsts[-1] = lax.optimization_barrier((came[p], firsts[-1]))
        firsts.append(0.5 * (part + (kept[p] + came[p])) / first_scale[p])
    held = [firsts]
    while bit > 1:
        bit //= 2
        swap = [(i, i ^ bit) for i in range(n_con)]
        block = [jnp.concatenate([h[p] for h in held], axis=1) if len(held) > 1 else held[0][p] for p in parts]
        held = held + [send(block[:-1], "con", swap) + send(block[-1:], "con", swap)]
    first_out = expand(jnp.concatenate(firsts, axis=0))
    late_other, _ = lax.optimization_barrier((other_second, firsts[-1]))
    second_other = cut(compact(late_other))
    *far, split = cols_sweep((n_res - 1, n_res), strip_tiles, integrals, held, fine, pieces=1, keeps=True)
    ahead = [lax.ppermute(far[p], "res", onward) if p < PARTS // 2 else None for p in parts]
    behind = [None if p < PARTS // 2 else lax.ppermute(far[p], "res", backward) for p in parts]
    for s in range(near - 1, 0, -1):
        edge = (2 * s - 1, 2 * s + 1)
        both = cols_sweep(edge, strip_tiles, integrals, None, 2 * fine, pieces=2, split=split)
        to_behind, to_ahead = both[:PARTS], both[PARTS:]
        ahead = send([to_ahead[p] if ahead[p] is None else to_ahead[p] + ahead[p] for p in parts], "res", onward)
        behind = send([to_behind[p] if behind[p] is None else to_behind[p] + behind[p] for p in parts], "res", backward)
    mine = cols_sweep((0, 1), strip_tiles, integrals, None, fine, pieces=1, split=split)
    seconds = [
        (0.5 * second_other[p] + ((mine[p] + ahead[p]) + behind[p])) / second_scale[p] for p in parts
    ]
    return first_out, expand(jnp.concatenate(seconds, axis=0))


def per_device(integrals, tile_mask, amplitudes, *rest):
    n_con = lax.axis_size("con")
    n_res = lax.axis_size("res")
    fits = (
        amplitudes.shape[0] % W == 0
        and amplitudes.shape[1] % (32 * PARTS) == 0
        and n_con & (n_con - 1) == 0
        and n_res % 2 == 0
        and n_res > 2
    )
    if not fits:
        return general(integrals, tile_mask, amplitudes, *rest)
    return tiled(integrals, tile_mask, amplitudes, *rest)


def solution(mesh):
    return jax.shard_map(
        per_device,
        mesh=mesh,
        in_specs=(
            P("res", "con"),
            P("res", "con"),
            P(("con", "res"), None),
            P(("res", "con"), None),
            P(("con", "res"), None),
            P(),
            P(),
            P(),
            P(),
            P(),
        ),
        out_specs=(P(("res", "con"), None), P(("con", "res"), None)),
        check_vma=False,
    )
```
